768 devices in a mesh: dp: 64 (over x, y, core), phase: 12 (over z).
Axes of the slice: x: 4, y: 8, z: 12, core: 2. Of those that a mesh axis runs over, the one named last changes fastest.
Arguments:
- patches: bfloat16 [98304, 1280], P(('dp', 'phase')), may hold values from -6 to 6
- window_ids: int32 [768, 128], P(('dp', 'phase')), may hold values from 0 to 3, never falling along the last dimension, each value on 1 to 64 neighbouring positions
- norm_gain: float32 [4, 1280], replicated, may hold values from 0.1 to 1.9
- w_qkv: bfloat16 [4, 1280, 1920], P(None, 'dp')
- w_out: bfloat16 [4, 640, 1280], P(None, 'dp'), may hold values from -0.25 to 0.25
- merge_gain: float32 [1280], replicated, may hold values from 0.1 to 1.9
Outputs:
- merged: bfloat16 [24576, 5120], P(('dp', 'phase'))
The draws below stay inside these ranges and needn't reach their ends.
Inputs may be any that keep to these rules, and one draw needn't show every extreme that they name: `window_ids`: window numbers never fall along a micro-batch; each window holds 1 to 64 patches, one exactly 64.
All inputs are finite; a program needn't handle non-finite values.
Results may differ from the reference program's by a relative error of at most 0.028.
Values may be sent and summed in bfloat16 or wider, within the bound.
A program may use at most 64 MiB of HBM per device.

```python
import math
import jax
import jax.numpy as jnp
import numpy as np
from jax import lax

D_VIS = 1280
HEADS = 8
HEAD_DIM = 80
MB = 128
SECTIONS = 4
WIN_MOST = 64
WINDOWS = 4
MICRO = 768


def draw_w_qkv(key, part):
    width = HEADS * HEAD_DIM
    base = jax.random.normal(key, (SECTIONS, D_VIS, 3 * width), jnp.float32) * D_VIS ** (-0.5)
    return base.astype(jnp.bfloat16)


def block_levels(stream_key, shape, shards, low, high):
    loudness, own = 1.0, jax.random.fold_in(stream_key, 6)
    for axis_at, blocks in shards:
        steps = jnp.exp(jax.random.uniform(jax.random.fold_in(own, axis_at), (blocks,), jnp.float32, low / len(shards), high / len(shards)))
        loudness = loudness * jnp.repeat(steps, shape[axis_at] // blocks).reshape([-1 if axis == axis_at else 1 for axis in range(len(shape))])
    return loudness


def length_profile(amount, total, reach, lean):
    loads = [(1 << 20) // math.isqrt(rank ** lean) + 1 for rank in range(2, amount + 1)]
    rest, given = total - reach - (amount - 1), [1] * (amount - 1)
    while rest > 0:
        movable = [i for i in range(amount - 1) if given[i] < reach]
        whole, remaining = sum([loads[i] for i in movable]), rest
        for i in movable:
            more = min(reach - given[i], max(1, remaining * loads[i] // whole), rest)
            given[i] = given[i] + more
            rest = rest - more
    return np.array([reach] + given)


def uneven(stream_key, count, total, limit, slope):
    if count == 2:
        one = jax.random.randint(stream_key, (), max(1, total - limit), min(limit, total - 1) + 1)
        return jnp.stack([one, total - one])
    lengths = jnp.asarray(length_profile(count, total, limit, slope), jnp.int32)
    twos = (count - 1) // 2
    donor, sink = lengths[1:1 + 2 * twos:2], lengths[2:2 + 2 * twos:2]
    margin = jnp.minimum(donor - 1, limit - sink)
    passed = jax.random.randint(jax.random.fold_in(stream_key, 1), (twos,), 0, 1 << 20) % (margin + 1)
    lengths = lengths.at[1:1 + 2 * twos:2].set(donor - passed).at[2:2 + 2 * twos:2].set(sink + passed)
    return lengths[jax.random.permutation(jax.random.fold_in(stream_key, 2), count)]


def gaussian(stream_key, dims, scale, bound, pieces=(), kind=jnp.bfloat16):
    result = jax.random.normal(stream_key, dims, jnp.float32) * scale
    if len(pieces) > 0:
        result = block_levels(stream_key, dims, pieces, -0.22, 0.18) * result
    return jnp.clip(result, min=-bound, max=bound).astype(kind)


def setup_inputs(seed: int = 0) -> dict:
    splits = jax.random.split(jax.random.key(seed), 7)
    patches = gaussian(splits[0], (MICRO * MB, D_VIS), 1.0, 6.0, ((0, 768),))
    window_ids = jax.vmap(lambda own: jnp.searchsorted(jnp.cumsum(uneven(own, WINDOWS, MB, WIN_MOST, 1)), jnp.arange(MB), side="right"))(jax.random.split(splits[1], MICRO)).reshape((MICRO, MB)).astype(jnp.int32)
    norm_gain = jnp.clip(1.0 + 0.18 * jax.random.normal(splits[2], (SECTIONS, D_VIS), jnp.float32), 0.1, 1.9)
    w_qkv = draw_w_qkv(jax.random.fold_in(splits[6], 71), 0)
    w_out = gaussian(splits[4], (SECTIONS, HEADS * HEAD_DIM, D_VIS), (HEADS * HEAD_DIM) ** -0.5, 0.25, ((1, 64),))
    merge_gain = jnp.clip(1.0 + 0.18 * jax.random.normal(splits[5], (D_VIS,), jnp.float32), 0.1, 1.9)
    return {"patches": patches, "window_ids": window_ids, "norm_gain": norm_gain, "w_qkv": w_qkv, "w_out": w_out, "merge_gain": merge_gain}


def rms_scale(values, gain):
    return values * lax.rsqrt(lax.optimization_barrier(jnp.mean(values * values, axis=-1, keepdims=True)) + 1e-06) * gain

def section(acts, window_ids, gain, weight_qkv, weight_out):
    width = HEADS * HEAD_DIM
    batch = acts.shape[0]
    values_f = acts.astype(jnp.float32)
    normed = rms_scale(values_f, gain).astype(jnp.bfloat16)
    qkv = jnp.einsum('bmd,de->bme', normed.astype(jnp.float32), weight_qkv.astype(jnp.float32)).astype(jnp.bfloat16)
    query = qkv[..., :width].reshape(batch, MB, HEADS, HEAD_DIM).astype(jnp.float32)
    keys = qkv[..., width:2 * width].reshape(batch, MB, HEADS, HEAD_DIM).astype(jnp.float32)
    vals = qkv[..., 2 * width:].reshape(batch, MB, HEADS, HEAD_DIM).astype(jnp.float32)
    scores = jnp.einsum('bqhd,bkhd->bhqk', query, keys) * HEAD_DIM ** (-0.5)
    same = window_ids[:, :, None] == window_ids[:, None, :]
    scores = jnp.where(same[:, None], scores, jnp.float32(-1e+30))
    highest = lax.optimization_barrier(jnp.max(scores, axis=-1, keepdims=True))
    weights = jnp.exp(scores - highest)
    probs = (weights / lax.optimization_barrier(jnp.sum(weights, axis=-1, keepdims=True))).astype(jnp.bfloat16)
    context = jnp.einsum('bhqk,bkhd->bqhd', probs.astype(jnp.float32), vals).astype(jnp.bfloat16)
    context = context.reshape(batch, MB, width)
    update = jnp.einsum('bme,ed->bmd', context.astype(jnp.float32), weight_out.astype(jnp.float32))
    return (values_f + update).astype(jnp.bfloat16)

def reference(patches, window_ids, norm_gain, w_qkv, w_out, merge_gain):
    acts = patches.reshape(-1, MB, D_VIS)
    for index in range(SECTIONS):
        acts = section(acts, window_ids, norm_gain[index], w_qkv[index], w_out[index])
    final = rms_scale(acts.reshape(-1, D_VIS).astype(jnp.float32), merge_gain).astype(jnp.bfloat16)
    return final.reshape(-1, 4 * D_VIS)
```

```python
import jax
import jax.numpy as jnp
from jax import lax
from jax.experimental import pallas as pl
from jax.experimental.pallas import tpu as pltpu
from jax.sharding import PartitionSpec as P

D_VIS = 1280
HEADS = 8
HEAD_DIM = 80
WIDTH = HEADS * HEAD_DIM
MB = 128
SECTIONS = 4
NX, NY = 4, 8
ROWS = 40
CA, CB = 384, 512
STEPS = 10
LAG = 2
MESH = pl.DeviceIdType.MESH


def rms(values, gain):
    return values * lax.rsqrt(jnp.mean(values * values, axis=-1, keepdims=True) + 1e-06) * gain


def kernel(
    block_a, block_b, patches, ids, gains, merge_gain, spread, out,
    wa, wb, acts, ctx, mask, tail,
    local_sem, ax, ay, az, by, bx, sib_a, sib_z, sib_b, sent,
):
    dp, z = lax.axis_index("dp"), lax.axis_index("phase")
    planes = lax.axis_size("phase")
    core = lax.rem(dp, 2)
    x, y = lax.div(dp, 2 * NY), lax.rem(lax.div(dp, 2), NY)
    half = lax.rem(z, 2)
    side = 1 - 2 * core

    def place(px, py, pc):
        return ((px * NY + py) * 2 + pc, z)

    def xs(d):
        return lax.rem(x + d + NX, NX)

    def ys(d):
        return lax.rem(y + d + NY, NY)

    east, west = place(xs(1), y, core), place(xs(-1), y, core)
    north, south = place(x, ys(1), core), place(x, ys(-1), core)
    up = (dp, lax.rem(z + 1, planes))
    down = (dp, lax.rem(z + planes - 1, planes))
    twin = place(x, y, 1 - core)
    x_side, y_side = place(xs(side), y, core), place(x, ys(side), core)

    def copy(ref, kind, recv, device):
        return pltpu.make_async_remote_copy(
            src_ref=ref, dst_ref=ref, send_sem=sent.at[kind], recv_sem=recv,
            device_id=device, device_id_type=MESH,
        )

    def send(ref, kind, recv, device):
        copy(ref, kind, recv, device).start()

    def arrive(ref, recv):
        copy(ref, 0, recv, twin).wait_recv()

    def drain(ref, kind):
        copy(ref, kind, local_sem.at[2], twin).wait_send()

    own_a = pltpu.make_async_copy(block_a.at[:, half], wa.at[core, :, half, x, y], local_sem.at[0])
    own_b = pltpu.make_async_copy(block_b, wb.at[core, :, x, y], local_sem.at[1])
    for item in (own_a, own_b):
        item.start()
    barrier = pltpu.get_barrier_semaphore()
    for device in (east, west, north, south, up, down, twin):
        pl.semaphore_signal(barrier, inc=1, device_id=device, device_id_type=MESH)

    marks = jnp.broadcast_to(ids[...].astype(jnp.float32), (MB, MB))
    mask[...] = jnp.where(marks == marks.T, jnp.float32(1), jnp.float32(0))
    acts[...] = patches[...]

    pl.semaphore_wait(barrier, 7)
    for item in (own_a, own_b):
        item.wait()

    def row_a(s, py):
        return wa.at[core, s, half, :, py]

    def spread_row(s, py):
        send(wa.at[core, s, half, 0:2, py], 2, az.at[s, 0], up)
        send(wa.at[core, s, half, 2:4, py], 2, az.at[s, 1], down)
        send(row_a(s, py), 3, sib_a.at[s], twin)

    def step_a(s, k):
        if k == 0:
            mine = wa.at[core, s, half, x, y]
            send(mine, 0, ax.at[s, 0], east)
            send(mine, 0, ax.at[s, 1], west)
        elif k == 1:
            arrive(wa.at[core, s, half, xs(-1), y], ax.at[s, 0])
            arrive(wa.at[core, s, half, xs(1), y], ax.at[s, 1])
            send(wa.at[core, s, half, xs(-side), y], 0, ax.at[s, 2], x_side)
        elif k == 2:
            arrive(wa.at[core, s, half, xs(2), y], ax.at[s, 2])
            send(row_a(s, y), 1, ay.at[s, 0], north)
            send(row_a(s, y), 1, ay.at[s, 1], south)
            spread_row(s, y)
        elif k in (3, 4, 5):
            d = k - 2
            arrive(row_a(s, ys(-d)), ay.at[s, 2 * d - 2])
            arrive(row_a(s, ys(d)), ay.at[s, 2 * d - 1])
            if d < 3:
                send(row_a(s, ys(-d)), 1, ay.at[s, 2 * d], north)
                send(row_a(s, ys(d)), 1, ay.at[s, 2 * d + 1], south)
            else:
                send(row_a(s, ys(-3 * side)), 1, ay.at[s, 6], y_side)
            spread_row(s, ys(-d))
            spread_row(s, ys(d))
        elif k == 6:
            arrive(row_a(s, ys(4)), ay.at[s, 6])
            spread_row(s, ys(4))
        elif k == 8:
            arrive(wa.at[core, s, 1 - half, 0:2], az.at[s, 0])
            arrive(wa.at[core, s, 1 - half, 2:4], az.at[s, 1])
            send(wa.at[core, s, 1 - half], 4, sib_z.at[s], twin)
        elif k == 9:
            arrive(wa.at[1 - core, s, half], sib_a.at[s])
            arrive(wa.at[1 - core, s, 1 - half], sib_z.at[s])

    def step_b(s, k):
        if k == 0:
            mine = wb.at[core, s, x, y]
            send(mine, 5, by.at[s, 0], north)
            send(mine, 5, by.at[s, 1], south)
        elif k in (1, 2, 3):
            d = k
            arrive(wb.at[core, s, x, ys(-d)], by.at[s, 2 * d - 2])
            arrive(wb.at[core, s, x, ys(d)], by.at[s, 2 * d - 1])
            if d < 3:
                send(wb.at[core, s, x, ys(-d)], 5, by.at[s, 2 * d], north)
                send(wb.at[core, s, x, ys(d)], 5, by.at[s, 2 * d + 1], south)
            else:
                send(wb.at[core, s, x, ys(-3 * side)], 5, by.at[s, 6], y_side)
        elif k == 4:
            arrive(wb.at[core, s, x, ys(4)], by.at[s, 6])
            send(wb.at[core, s, x], 6, bx.at[s, 0], east)
            send(wb.at[core, s, x], 6, bx.at[s, 1], west)
            send(wb.at[core, s, x], 7, sib_b.at[s], twin)
        elif k == 6:
            arrive(wb.at[core, s, xs(-1)], bx.at[s, 0])
            arrive(wb.at[core, s, xs(1)], bx.at[s, 1])
            send(wb.at[core, s, xs(-side)], 6, bx.at[s, 2], x_side)
            send(wb.at[core, s, xs(-1)], 7, sib_b.at[s], twin)
            send(wb.at[core, s, xs(1)], 7, sib_b.at[s], twin)
        elif k == 8:
            arrive(wb.at[core, s, xs(2)], bx.at[s, 2])
            send(wb.at[core, s, xs(2)], 7, sib_b.at[s], twin)
        elif k == 9:
            arrive(wb.at[1 - core, s], sib_b.at[s])

    for tick in range(LAG * (SECTIONS - 1) + STEPS):
        for s in range(SECTIONS):
            k = tick - LAG * s
            if 0 <= k < STEPS:
                step_a(s, k)
                step_b(s, k)

    drain(wa.at[0, :, 0, 0:3, 0], 0)
    drain(wa.at[0, :, 0, :, 0:7], 1)
    drain(wa.at[0, :, 0], 2)
    drain(wa.at[0, :, 0], 3)
    drain(wa.at[0, :, 0], 4)
    drain(wb.at[0, :, 0, 0:7], 5)
    drain(wb.at[0, :, 0:3], 6)
    drain(wb.at[0], 7)

    def weight_a(lane, s, h):
        return wa[lane, s, h].reshape(D_VIS, CA)

    def weight_b(lane, s):
        return wb[lane, s].reshape(D_VIS, CB)

    def dot(a, b):
        return jnp.dot(a, b, preferred_element_type=jnp.float32)

    lanes = lax.broadcasted_iota(jnp.int32, (1, 256), 1)

    def section(s, carry):
        values = acts[...].astype(jnp.float32)
        normed = rms(values, gains[pl.ds(s, 1), :]).astype(jnp.bfloat16)
        qk = [
            dot(normed, weight_a(0, s, 0)), dot(normed, weight_a(0, s, 1)), dot(normed, weight_b(0, s)),
        ]
        qk = jnp.concatenate([item.astype(jnp.bfloat16) for item in qk], axis=1)
        v0 = dot(normed, weight_a(1, s, 0)).astype(jnp.bfloat16)
        v1 = dot(normed, wa[1, s, 1, :, :, :, 0:256].reshape(D_VIS, 256)).astype(jnp.bfloat16)
        vals = dot(jnp.concatenate([v0, v1], axis=1), spread[...]).astype(jnp.bfloat16)
        same = mask[...] > 0
        ctx[...] = jnp.zeros_like(ctx)
        for head in range(HEADS):
            lo = head * HEAD_DIM
            base = lo // 128 * 128
            wide = min(256, WIDTH - base)
            here = (lanes[:, :wide] >= lo - base) & (lanes[:, :wide] < lo - base + HEAD_DIM)
            query = jnp.where(here, qk[:, base : base + wide], jnp.bfloat16(0))
            keys = qk[:, WIDTH + base : WIDTH + base + wide]
            scores = lax.dot_general(
                query, keys, (((1,), (1,)), ((), ())), preferred_element_type=jnp.float32
            ) * HEAD_DIM ** (-0.5)
            scores = jnp.where(same, scores, jnp.float32(-1e30))
            weights = jnp.exp(scores - jnp.max(scores, axis=-1, keepdims=True))
            probs = (weights / jnp.sum(weights, axis=-1, keepdims=True)).astype(jnp.bfloat16)
            lo = head * 2 * HEAD_DIM
            base = lo // 128 * 128
            here = (lanes >= lo - base) & (lanes < lo - base + 2 * HEAD_DIM)
            part = dot(probs, jnp.where(here, vals[:, base : base + 256], jnp.bfloat16(0)))
            ctx[:, base : base + 256] += part
        first = ctx[...]
        second = pltpu.roll(first, 10, 1)
        both = jnp.concatenate([first.astype(jnp.bfloat16), second.astype(jnp.bfloat16)], axis=0)
        o0 = dot(both, wa[1, s, 1, :, :, :, 256:384].reshape(D_VIS, 128))
        o1 = dot(both, weight_b(1, s))
        update = jnp.concatenate(
            [jnp.concatenate([o0[r : r + MB], o1[r : r + MB]], axis=1) for r in (0, MB)], axis=1
        )
        acts[...] = (values + update).astype(jnp.bfloat16)
        return carry

    lax.fori_loop(0, SECTIONS, section, 0)

    final = rms(acts[...].astype(jnp.float32), merge_gain[...])
    for i in range(D_VIS // 128):
        tail[i * MB : (i + 1) * MB, :] = final[:, i * 128 : (i + 1) * 128]
    for j in range(4):
        for i in range(D_VIS // 128):
            rows = tail[pl.ds(i * MB + j, MB // 4, stride=4), :]
            out[:, j * D_VIS + i * 128 : j * D_VIS + (i + 1) * 128] = rows.astype(jnp.bfloat16)


def body(patches, window_ids, norm_gain, w_qkv, w_out, merge_gain):
    core = lax.axis_index("dp") % 2
    count = w_qkv.shape[0]
    qk = w_qkv[:, :, : 2 * WIDTH]
    rows_o = w_out.shape[1]
    halves = jnp.concatenate([w_out[:, :, :WIDTH], w_out[:, :, WIDTH:]], axis=1)
    vo = jnp.concatenate([w_qkv[:, :, 2 * WIDTH :], halves], axis=2)
    swap = [(i, i ^ 1) for i in range(lax.axis_size("dp"))]
    got = lax.ppermute(jnp.where(core == 0, vo, qk), "dp", swap)
    block = jnp.where(
        core == 0, jnp.concatenate([qk, got], axis=1), jnp.concatenate([got, vo], axis=1)
    )
    block_a = jnp.stack([block[:, :, :CA], block[:, :, CA : 2 * CA]], axis=1)
    block_b = block[:, :, 2 * CA :]
    place = jnp.arange(2 * WIDTH)[None, :]
    source = jnp.arange(WIDTH)[:, None]
    spread = ((place % 20 < 10) & (place // 20 * 10 + place % 20 == source)).astype(jnp.bfloat16)
    vmem = pl.BlockSpec(memory_space=pltpu.VMEM)
    hbm = pl.BlockSpec(memory_space=pl.ANY)
    dma = pltpu.SemaphoreType.DMA
    return pl.pallas_call(
        kernel,
        out_shape=jax.ShapeDtypeStruct((MB // 4, 4 * D_VIS), jnp.bfloat16),
        in_specs=[hbm, hbm] + [vmem] * 5,
        out_specs=vmem,
        scratch_shapes=[
            pltpu.VMEM((2, SECTIONS, 2, NX, NY, ROWS, CA), jnp.bfloat16),
            pltpu.VMEM((2, SECTIONS, NX, NY, ROWS, CB), jnp.bfloat16),
            pltpu.VMEM((MB, D_VIS), jnp.bfloat16),
            pltpu.VMEM((MB, 2 * WIDTH), jnp.float32),
            pltpu.VMEM((MB, MB), jnp.float32),
            pltpu.VMEM((D_VIS // 128 * MB, 128), jnp.float32),
            dma((3,)),
            dma((SECTIONS, 3)),
            dma((SECTIONS, 7)),
            dma((SECTIONS, 2)),
            dma((SECTIONS, 7)),
            dma((SECTIONS, 3)),
            dma((SECTIONS,)),
            dma((SECTIONS,)),
            dma((SECTIONS,)),
            dma((8,)),
        ],
        compiler_params=pltpu.CompilerParams(
            collective_id=0, has_side_effects=True, vmem_limit_bytes=60 * 1024 * 1024
        ),
    )(block_a, block_b, patches, window_ids, norm_gain, merge_gain.reshape(1, D_VIS), spread)


def solution(mesh):
    in_specs = (
        P(("dp", "phase"), None),
        P(("dp", "phase"), None),
        P(),
        P(None, "dp", None),
        P(None, "dp", None),
        P(),
    )
    out_specs = P(("dp", "phase"), None)
    return jax.shard_map(body, mesh=mesh, in_specs=in_specs, out_specs=out_specs, check_vma=False)
```

```python
import jax
import jax.numpy as jnp
from jax import lax
from jax.experimental import pallas as pl
from jax.experimental.pallas import tpu as pltpu
from jax.sharding import PartitionSpec as P

D_VIS = 1280
HEADS = 8
HEAD_DIM = 80
WIDTH = HEADS * HEAD_DIM
MB = 128
SECTIONS = 4
NX, NY = 4, 8
ROWS = 40
CA, CB = 384, 512
STEPS = 10
LAG = 2
MESH = pl.DeviceIdType.MESH


def rms(values, gain):
    return values * lax.rsqrt(jnp.mean(values * values, axis=-1, keepdims=True) + 1e-06) * gain


def kernel(
    block_a, block_b, patches, ids, gains, merge_gain, out,
    wa, wb, acts, ctx, mask, tail, spread,
    local_sem, ax, ay, az, by, bx, sib_a, sib_z, sib_b, sent,
):
    dp, z = lax.axis_index("dp"), lax.axis_index("phase")
    planes = lax.axis_size("phase")
    core = lax.rem(dp, 2)
    x, y = lax.div(dp, 2 * NY), lax.rem(lax.div(dp, 2), NY)
    half = lax.rem(z, 2)
    side = 1 - 2 * core

    def place(px, py, pc):
        return ((px * NY + py) * 2 + pc, z)

    def xs(d):
        return lax.rem(x + d + NX, NX)

    def ys(d):
        return lax.rem(y + d + NY, NY)

    east, west = place(xs(1), y, core), place(xs(-1), y, core)
    north, south = place(x, ys(1), core), place(x, ys(-1), core)
    up = (dp, lax.rem(z + 1, planes))
    down = (dp, lax.rem(z + planes - 1, planes))
    twin = place(x, y, 1 - core)
    x_side, y_side = place(xs(side), y, core), place(x, ys(side), core)

    def copy(ref, kind, recv, device):
        return pltpu.make_async_remote_copy(
            src_ref=ref, dst_ref=ref, send_sem=sent.at[kind], recv_sem=recv,
            device_id=device, device_id_type=MESH,
        )

    def send(ref, kind, recv, device):
        copy(ref, kind, recv, device).start()

    def arrive(ref, recv):
        copy(ref, 0, recv, twin).wait_recv()

    def drain(ref, kind):
        copy(ref, kind, local_sem.at[2], twin).wait_send()

    own_a = pltpu.make_async_copy(block_a.at[:, half], wa.at[core, :, half, x, y], local_sem.at[0])
    own_b = pltpu.make_async_copy(block_b, wb.at[core, :, x, y], local_sem.at[1])
    for item in (own_a, own_b):
        item.start()
    barrier = pltpu.get_barrier_semaphore()
    for device in (east, west, north, south, up, down, twin):
        pl.semaphore_signal(barrier, inc=1, device_id=device, device_id_type=MESH)

    marks = jnp.broadcast_to(ids[...].astype(jnp.float32), (MB, MB))
    mask[...] = jnp.where(marks == marks.T, jnp.float32(1), jnp.float32(0))
    acts[...] = patches[...]

    pl.semaphore_wait(barrier, 7)
    for item in (own_a, own_b):
        item.wait()

    def row_a(s, py):
        return wa.at[core, s, half, :, py]

    def spread_row(s, py):
        send(wa.at[core, s, half, 0:2, py], 2, az.at[s, 0], up)
        send(wa.at[core, s, half, 2:4, py], 2, az.at[s, 1], down)
        send(row_a(s, py), 3, sib_a.at[s], twin)

    def step_a(s, k):
        if k == 0:
            mine = wa.at[core, s, half, x, y]
            send(mine, 0, ax.at[s, 0], east)
            send(mine, 0, ax.at[s, 1], west)
        elif k == 1:
            arrive(wa.at[core, s, half, xs(-1), y], ax.at[s, 0])
            arrive(wa.at[core, s, half, xs(1), y], ax.at[s, 1])
            send(wa.at[core, s, half, xs(-side), y], 0, ax.at[s, 2], x_side)
        elif k == 2:
            arrive(wa.at[core, s, half, xs(2), y], ax.at[s, 2])
            send(row_a(s, y), 1, ay.at[s, 0], north)
            send(row_a(s, y), 1, ay.at[s, 1], south)
            spread_row(s, y)
        elif k in (3, 4, 5):
            d = k - 2
            arrive(row_a(s, ys(-d)), ay.at[s, 2 * d - 2])
            arrive(row_a(s, ys(d)), ay.at[s, 2 * d - 1])
            if d < 3:
                send(row_a(s, ys(-d)), 1, ay.at[s, 2 * d], north)
                send(row_a(s, ys(d)), 1, ay.at[s, 2 * d + 1], south)
            else:
                send(row_a(s, ys(-3 * side)), 1, ay.at[s, 6], y_side)
            spread_row(s, ys(-d))
            spread_row(s, ys(d))
        elif k == 6:
            arrive(row_a(s, ys(4)), ay.at[s, 6])
            spread_row(s, ys(4))
        elif k == 8:
            arrive(wa.at[core, s, 1 - half, 0:2], az.at[s, 0])
            arrive(wa.at[core, s, 1 - half, 2:4], az.at[s, 1])
            send(wa.at[core, s, 1 - half], 4, sib_z.at[s], twin)
        elif k == 9:
            arrive(wa.at[1 - core, s, half], sib_a.at[s])
            arrive(wa.at[1 - core, s, 1 - half], sib_z.at[s])

    def step_b(s, k):
        if k == 0:
            mine = wb.at[core, s, x, y]
            send(mine, 5, by.at[s, 0], north)
            send(mine, 5, by.at[s, 1], south)
        elif k in (1, 2, 3):
            d = k
            arrive(wb.at[core, s, x, ys(-d)], by.at[s, 2 * d - 2])
            arrive(wb.at[core, s, x, ys(d)], by.at[s, 2 * d - 1])
            if d < 3:
                send(wb.at[core, s, x, ys(-d)], 5, by.at[s, 2 * d], north)
                send(wb.at[core, s, x, ys(d)], 5, by.at[s, 2 * d + 1], south)
            else:
                send(wb.at[core, s, x, ys(-3 * side)], 5, by.at[s, 6], y_side)
        elif k == 4:
            arrive(wb.at[core, s, x, ys(4)], by.at[s, 6])
            send(wb.at[core, s, x], 6, bx.at[s, 0], east)
            send(wb.at[core, s, x], 6, bx.at[s, 1], west)
            send(wb.at[core, s, x], 7, sib_b.at[s], twin)
        elif k == 6:
            arrive(wb.at[core, s, xs(-1)], bx.at[s, 0])
            arrive(wb.at[core, s, xs(1)], bx.at[s, 1])
            send(wb.at[core, s, xs(-side)], 6, bx.at[s, 2], x_side)
            send(wb.at[core, s, xs(-1)], 7, sib_b.at[s], twin)
            send(wb.at[core, s, xs(1)], 7, sib_b.at[s], twin)
        elif k == 8:
            arrive(wb.at[core, s, xs(2)], bx.at[s, 2])
            send(wb.at[core, s, xs(2)], 7, sib_b.at[s], twin)
        elif k == 9:
            arrive(wb.at[1 - core, s], sib_b.at[s])

    def tick(t):
        for s in range(SECTIONS):
            k = t - LAG * s
            if 0 <= k < STEPS:
                step_a(s, k)
                step_b(s, k)

    def later(s, t):
        for j in range(1, SECTIONS):
            k = t - LAG * j

            @pl.when(s + j < SECTIONS)
            def _():
                step_a(s + j, k)
                step_b(s + j, k)

    tick(0)
    column = lax.broadcasted_iota(jnp.int32, (1, 2 * WIDTH), 1)
    inner = lax.rem(column, 20)
    source = jnp.where(inner < 10, lax.div(column, 20) * 10 + inner, -1)

    def spread_rows(i, carry):
        row = lax.broadcasted_iota(jnp.int32, (64, 2 * WIDTH), 0) + i * 64
        spread[pl.ds(pl.multiple_of(i * 64, 64), 64), :] = jnp.where(
            row == source, jnp.float32(1), jnp.float32(0)
        ).astype(jnp.bfloat16)
        return carry

    lax.fori_loop(0, WIDTH // 64, spread_rows, 0)
    for t in range(1, STEPS):
        tick(t)

    def weight_a(lane, s, h):
        return wa[lane, s, h].reshape(D_VIS, CA)

    def weight_b(lane, s):
        return wb[lane, s].reshape(D_VIS, CB)

    def dot(a, b):
        return jnp.dot(a, b, preferred_element_type=jnp.float32)

    lanes = lax.broadcasted_iota(jnp.int32, (1, 256), 1)

    def section(s, carry):
        values = acts[...].astype(jnp.float32)
        normed = rms(values, gains[pl.ds(s, 1), :]).astype(jnp.bfloat16)
        qk = [
            dot(normed, weight_a(0, s, 0)), dot(normed, weight_a(0, s, 1)), dot(normed, weight_b(0, s)),
        ]
        qk = jnp.concatenate([item.astype(jnp.bfloat16) for item in qk], axis=1)
        v0 = dot(normed, weight_a(1, s, 0)).astype(jnp.bfloat16)
        v1 = dot(normed, wa[1, s, 1, :, :, :, 0:256].reshape(D_VIS, 256)).astype(jnp.bfloat16)
        vals = dot(jnp.concatenate([v0, v1], axis=1), spread[...]).astype(jnp.bfloat16)
        later(s, STEPS)
        same = mask[...] > 0
        ctx[...] = jnp.zeros_like(ctx)
        for head in range(HEADS):
            lo = head * HEAD_DIM
            base = lo // 128 * 128
            wide = min(256, WIDTH - base)
            here = (lanes[:, :wide] >= lo - base) & (lanes[:, :wide] < lo - base + HEAD_DIM)
            query = jnp.where(here, qk[:, base : base + wide], jnp.bfloat16(0))
            keys = qk[:, WIDTH + base : WIDTH + base + wide]
            scores = lax.dot_general(
                query, keys, (((1,), (1,)), ((), ())), preferred_element_type=jnp.float32
            ) * HEAD_DIM ** (-0.5)
            scores = jnp.where(same, scores, jnp.float32(-1e30))
            weights = jnp.exp(scores - jnp.max(scores, axis=-1, keepdims=True))
            probs = (weights / jnp.sum(weights, axis=-1, keepdims=True)).astype(jnp.bfloat16)
            lo = head * 2 * HEAD_DIM
            base = lo // 128 * 128
            here = (lanes >= lo - base) & (lanes < lo - base + 2 * HEAD_DIM)
            part = dot(probs, jnp.where(here, vals[:, base : base + 256], jnp.bfloat16(0)))
            ctx[:, base : base + 256] += part
        first = ctx[...]
        second = pltpu.roll(first, 10, 1)
        both = jnp.concatenate([first.astype(jnp.bfloat16), second.astype(jnp.bfloat16)], axis=0)
        o0 = dot(both, wa[1, s, 1, :, :, :, 256:384].reshape(D_VIS, 128))
        o1 = dot(both, weight_b(1, s))
        update = jnp.concatenate(
            [jnp.concatenate([o0[r : r + MB], o1[r : r + MB]], axis=1) for r in (0, MB)], axis=1
        )
        acts[...] = (values + update).astype(jnp.bfloat16)
        later(s, STEPS + 1)
        return carry

    lax.fori_loop(0, SECTIONS, section, 0)

    drain(wa.at[0, :, 0, 0:3, 0], 0)
    drain(wa.at[0, :, 0, :, 0:7], 1)
    drain(wa.at[0, :, 0], 2)
    drain(wa.at[0, :, 0], 3)
    drain(wa.at[0, :, 0], 4)
    drain(wb.at[0, :, 0, 0:7], 5)
    drain(wb.at[0, :, 0:3], 6)
    drain(wb.at[0], 7)

    final = rms(acts[...].astype(jnp.float32), merge_gain[...])
    for i in range(D_VIS // 128):
        tail[i * MB : (i + 1) * MB, :] = final[:, i * 128 : (i + 1) * 128]
    for j in range(4):
        for i in range(D_VIS // 128):
            rows = tail[pl.ds(i * MB + j, MB // 4, stride=4), :]
            out[:, j * D_VIS + i * 128 : j * D_VIS + (i + 1) * 128] = rows.astype(jnp.bfloat16)


def body(patches, window_ids, norm_gain, w_qkv, w_out, merge_gain):
    core = lax.axis_index("dp") % 2
    count = w_qkv.shape[0]
    qk = w_qkv[:, :, : 2 * WIDTH]
    rows_o = w_out.shape[1]
    halves = jnp.concatenate([w_out[:, :, :WIDTH], w_out[:, :, WIDTH:]], axis=1)
    vo = jnp.concatenate([w_qkv[:, :, 2 * WIDTH :], halves], axis=2)
    swap = [(i, i ^ 1) for i in range(lax.axis_size("dp"))]
    got = lax.ppermute(jnp.where(core == 0, vo, qk), "dp", swap)
    block = jnp.where(
        core == 0, jnp.concatenate([qk, got], axis=1), jnp.concatenate([got, vo], axis=1)
    )
    block_a = jnp.stack([block[:, :, :CA], block[:, :, CA : 2 * CA]], axis=1)
    block_b = block[:, :, 2 * CA :]
    vmem = pl.BlockSpec(memory_space=pltpu.VMEM)
    hbm = pl.BlockSpec(memory_space=pl.ANY)
    dma = pltpu.SemaphoreType.DMA
    return pl.pallas_call(
        kernel,
        out_shape=jax.ShapeDtypeStruct((MB // 4, 4 * D_VIS), jnp.bfloat16),
        in_specs=[hbm, hbm] + [vmem] * 4,
        out_specs=vmem,
        scratch_shapes=[
            pltpu.VMEM((2, SECTIONS, 2, NX, NY, ROWS, CA), jnp.bfloat16),
            pltpu.VMEM((2, SECTIONS, NX, NY, ROWS, CB), jnp.bfloat16),
            pltpu.VMEM((MB, D_VIS), jnp.bfloat16),
            pltpu.VMEM((MB, 2 * WIDTH), jnp.float32),
            pltpu.VMEM((MB, MB), jnp.float32),
            pltpu.VMEM((D_VIS // 128 * MB, 128), jnp.float32),
            pltpu.VMEM((WIDTH, 2 * WIDTH), jnp.bfloat16),
            dma((3,)),
            dma((SECTIONS, 3)),
            dma((SECTIONS, 7)),
            dma((SECTIONS, 2)),
            dma((SECTIONS, 7)),
            dma((SECTIONS, 3)),
            dma((SECTIONS,)),
            dma((SECTIONS,)),
            dma((SECTIONS,)),
            dma((8,)),
        ],
        compiler_params=pltpu.CompilerParams(
            collective_id=0, has_side_effects=True, vmem_limit_bytes=60 * 1024 * 1024
        ),
    )(block_a, block_b, patches, window_ids, norm_gain, merge_gain.reshape(1, D_VIS))


def solution(mesh):
    in_specs = (
        P(("dp", "phase"), None),
        P(("dp", "phase"), None),
        P(),
        P(None, "dp", None),
        P(None, "dp", None),
        P(),
    )
    out_specs = P(("dp", "phase"), None)
    return jax.shard_map(body, mesh=mesh, in_specs=in_specs, out_specs=out_specs, check_vma=False)
```
